32 devices in a mesh: ctx: 8 (over z, x), head: 4 (over y, core).
Axes of the slice: x: 2, y: 2, z: 4, core: 2. Of those that a mesh axis runs over, the one named last changes fastest.
Arguments:
- query_in: bfloat16 [1024, 8192], P('ctx', 'head'), may hold values from -6 to 6
- key_in: bfloat16 [1024, 8192], P('ctx', 'head'), may hold values from -6 to 6
- value_in: bfloat16 [1024, 8192], P('ctx', 'head'), may hold values from -12 to 12
- conv_taps: float32 [3, 4, 8192], P(None, None, 'head'), may hold values from -3 to 3
- norm_gain: float32 [8192], P('head'), may hold values from 0.25 to 1.75
- cotangent: bfloat16 [1024, 8192], P('ctx', 'head'), may hold values from -6 to 6
Outputs:
- attended: bfloat16 [1024, 8192], P('ctx', 'head')
- grad_query: bfloat16 [1024, 8192], P('ctx', 'head')
- grad_key: bfloat16 [1024, 8192], P('ctx', 'head')
- grad_value: bfloat16 [1024, 8192], P('ctx', 'head')
- grad_taps: float32 [3, 4, 8192], P(None, None, 'head')
- grad_gain: float32 [8192], P('head')
The draws below stay inside these ranges and needn't reach their ends.
All inputs are finite; a program needn't handle non-finite values.
Results may differ from the reference program's by a relative error of at most 0.0074.
Values may be sent and summed in bfloat16 or wider, within the bound.
A program may use at most 192 MiB of HBM per device.

```python
import math
import jax
import jax.numpy as jnp
from jax import lax

H = 64
DH = 128
W = 8192
KS = 4
TOK_DEV = 128
TOKENS = 1024
N_CTX = 8


def draw_value_in(key, part):
    draw_key, second = jax.random.split(key)
    position = jnp.arange(W, dtype=jnp.float32) / (W - 1)
    rough = jax.random.uniform(second, (W,), jnp.float32, 0.7, 1.4)
    baseline = 0.8 * jnp.power(1.7320508, position)
    values = jnp.clip(jax.random.normal(draw_key, (TOKENS, W), jnp.float32), -6.0, 6.0)
    return (values * baseline * rough).astype(jnp.bfloat16)


def block_scale(own_key, shape, shards, least, largest):
    loudness = 1.0
    for dim, shards_of in shards:
        steps = jax.random.uniform(jax.random.fold_in(jax.random.fold_in(own_key, 6), dim), (shards_of,), jnp.float32, least / len(shards), largest / len(shards))
        loudness = loudness * jnp.repeat(jnp.exp(steps), shape[dim] // shards_of).reshape((-1,) + (1,) * (len(shape) - 1 - dim))
    return loudness


def normal_values(stream_key, extent, deviation, most, shards=(), kind=jnp.bfloat16):
    gain = block_scale(stream_key, extent, shards, -0.22, 0.18) if shards else 1.0
    drawn = jax.random.normal(stream_key, extent, jnp.float32) * deviation * gain
    return jnp.minimum(jnp.maximum(drawn, -most), most).astype(kind)


def setup_inputs(seed: int = 0) -> dict:
    splits = jax.random.split(jax.random.key(seed), 7)
    return {
        "query_in": normal_values(splits[0], (TOKENS, W), 1.0, 6.0, ((0, 8), (1, 4))),
        "key_in": normal_values(splits[1], (TOKENS, W), 1.0, 6.0, ((0, 8), (1, 4))),
        "value_in": draw_value_in(jax.random.fold_in(splits[6], 71), 0),
        "conv_taps": normal_values(splits[3], (3, KS, W), 0.5, 3.0, ((2, 4),), jnp.float32),
        "norm_gain": jnp.clip(1.0 + 0.15 * jax.random.normal(splits[4], (W,), jnp.float32), 0.25, 1.75),
        "cotangent": normal_values(splits[5], (TOKENS, W), 1.0, 6.0, ((0, 8), (1, 4))),
    }


epsilon = 1e-06

def widened(source):
    return source.astype(jnp.float32)

def conv_rows(padded, taps):
    row_count = padded.shape[0] - (KS - 1)
    summed = jnp.zeros((row_count, padded.shape[1]), jnp.float32)
    for offset in range(KS):
        summed = summed + taps[offset] * padded[offset:offset + row_count].astype(jnp.float32)
    return summed

def conv_back(extended, taps):
    row_count = extended.shape[0] - (KS - 1)
    summed = jnp.zeros((row_count, extended.shape[1]), jnp.float32)
    for offset in range(KS):
        first_row = KS - 1 - offset
        summed = summed + taps[offset] * extended[first_row:first_row + row_count]
    return summed

def taps_grad(gradient, padded):
    row_count = gradient.shape[0]
    return jnp.stack([lax.optimization_barrier(jnp.sum(gradient * padded[offset:offset + row_count].astype(jnp.float32), axis=0)) for offset in range(KS)])

def silu_slope(preact):
    sigmoid_val = jax.nn.sigmoid(preact)
    return sigmoid_val * (1.0 + preact * (1.0 - sigmoid_val))

def as_heads(source):
    return source.reshape(source.shape[0], source.shape[1] // DH, DH)

def reference(query_in, key_in, value_in, conv_taps, norm_gain, cotangent):
    edge_rows = KS - 1
    padded_all = [jnp.pad(source, ((edge_rows, 0), (0, 0))) for source in (query_in, key_in, value_in)]
    group_ids = jnp.arange(N_CTX, dtype=jnp.int32)
    causal = jnp.arange(TOK_DEV)[:, None] >= jnp.arange(TOK_DEV)[None, :]

    def pieces(group_index):
        first_row = (group_index * TOK_DEV).astype(jnp.int32)
        return [lax.dynamic_slice_in_dim(source, first_row, TOK_DEV + edge_rows, 0) for source in padded_all]

    def featurize(padded):
        pre_query = conv_rows(padded[0], conv_taps[0])
        pre_key = conv_rows(padded[1], conv_taps[1])
        pre_value = conv_rows(padded[2], conv_taps[2])
        query_feat = jax.nn.silu(pre_query).astype(jnp.bfloat16)
        key_feat = jax.nn.silu(pre_key).astype(jnp.bfloat16)
        value_feat = pre_value.astype(jnp.bfloat16)
        return (pre_query, pre_key, query_feat, key_feat, value_feat)

    def scores_of(query_heads, key_heads):
        scores = jnp.einsum('thd,shd->hts', widened(query_heads), widened(key_heads))
        return jnp.where(causal[None], scores, 0.0).astype(jnp.bfloat16)

    def first_pass(carried_state, group_index):
        padded = pieces(group_index)
        _, _, _, key_feat, value_feat = featurize(padded)
        local_state = jnp.einsum('thd,the->hde', widened(as_heads(key_feat)), widened(as_heads(value_feat)))
        return (carried_state + local_state, carried_state.astype(jnp.bfloat16))
    zero_state = jnp.zeros((H, DH, DH), jnp.float32)
    _, earlier_all = lax.scan(first_pass, zero_state, group_ids)

    def second_pass(unused, inputs):
        group_index, earlier_b = inputs
        padded = pieces(group_index)
        _, _, query_feat, key_feat, value_feat = featurize(padded)
        query_heads = as_heads(query_feat)
        value_heads = as_heads(value_feat)
        weights_b = scores_of(query_heads, as_heads(key_feat))
        within = jnp.einsum('hts,shd->thd', widened(weights_b), widened(value_heads))
        carried = jnp.einsum('thd,hde->the', widened(query_heads), widened(earlier_b))
        mixed = (within + carried).reshape(TOK_DEV, W)
        inverse = lax.rsqrt(lax.optimization_barrier(jnp.mean(mixed * mixed, axis=1, keepdims=True)) + epsilon)
        attended = (mixed * inverse * norm_gain).astype(jnp.bfloat16)
        grad_up = widened(lax.dynamic_slice_in_dim(cotangent, (group_index * TOK_DEV).astype(jnp.int32), TOK_DEV, 0))
        scaled = norm_gain * grad_up
        dotted = lax.optimization_barrier(jnp.mean(scaled * mixed, axis=1, keepdims=True))
        grad_mixed = (inverse * scaled - mixed * inverse ** 3 * dotted).astype(jnp.bfloat16)
        gain_part = lax.optimization_barrier(jnp.sum(grad_up * mixed * inverse, axis=0))
        query_state = jnp.einsum('thd,the->hde', widened(query_heads), widened(as_heads(grad_mixed)))
        return (unused, (attended, grad_mixed, gain_part, query_state))
    _, (attended_all, grad_mixed_all, gain_parts, query_states) = lax.scan(second_pass, jnp.zeros((), jnp.float32), (group_ids, earlier_all))

    def third_pass(carry, inputs):
        later_sum, ahead_rows = carry
        group_index, earlier_b, grad_mixed, query_state = inputs
        padded = pieces(group_index)
        pre_query, pre_key, query_feat, key_feat, value_feat = featurize(padded)
        query_heads = as_heads(query_feat)
        key_heads = as_heads(key_feat)
        value_heads = as_heads(value_feat)
        grad_heads = as_heads(grad_mixed)
        weights_b = scores_of(query_heads, key_heads)
        later_b = later_sum.astype(jnp.bfloat16)
        grad_scores = jnp.einsum('the,she->hts', widened(grad_heads), widened(value_heads))
        grad_weights = jnp.where(causal[None], grad_scores, 0.0).astype(jnp.bfloat16)
        grad_qf = jnp.einsum('hts,shd->thd', widened(grad_weights), widened(key_heads)) + jnp.einsum('the,hde->thd', widened(grad_heads), widened(earlier_b))
        grad_kf = jnp.einsum('hts,thd->shd', widened(grad_weights), widened(query_heads)) + jnp.einsum('she,hde->shd', widened(value_heads), widened(later_b))
        grad_vf = jnp.einsum('hts,the->she', widened(weights_b), widened(grad_heads)) + jnp.einsum('shd,hde->she', widened(key_heads), widened(later_b))
        grads_pre = [grad_qf.reshape(TOK_DEV, W) * silu_slope(pre_query), grad_kf.reshape(TOK_DEV, W) * silu_slope(pre_key), grad_vf.reshape(TOK_DEV, W)]
        grads_in = []
        taps_parts = []
        for member in range(3):
            extended = jnp.concatenate([grads_pre[member], ahead_rows[member]], axis=0)
            grads_in.append(conv_back(extended, conv_taps[member]).astype(jnp.bfloat16))
            taps_parts.append(taps_grad(grads_pre[member], padded[member]))
        leading = jnp.stack([gradient[:edge_rows] for gradient in grads_pre])
        return ((later_sum + query_state, leading), (grads_in[0], grads_in[1], grads_in[2], jnp.stack(taps_parts)))
    start_carry = (zero_state, jnp.zeros((3, edge_rows, W), jnp.float32))
    _, (grad_q_all, grad_k_all, grad_v_all, taps_all) = lax.scan(third_pass, start_carry, (group_ids, earlier_all, grad_mixed_all, query_states), reverse=True)
    scale = 1.0 / math.sqrt(TOKENS)
    attended = attended_all.reshape(TOKENS, W)
    grad_query = grad_q_all.reshape(TOKENS, W)
    grad_key = grad_k_all.reshape(TOKENS, W)
    grad_value = grad_v_all.reshape(TOKENS, W)
    grad_taps = lax.optimization_barrier(jnp.sum(taps_all, axis=0)) * scale
    grad_gain = lax.optimization_barrier(jnp.sum(gain_parts, axis=0)) * scale
    return (attended, grad_query, grad_key, grad_value, grad_taps, grad_gain)
```

```python
import functools
import math

import jax
import jax.numpy as jnp
from jax import lax
from jax.experimental import pallas as pl
from jax.experimental.pallas import tpu as pltpu
from jax.sharding import PartitionSpec as P

DH = 128
W = 8192
KS = 4
GROUP = 2
TAIL = 8
EPSILON = 1e-06

f32 = jnp.float32
bf16 = jnp.bfloat16
MESH = pl.DeviceIdType.MESH


def dot(a, b, da, db):
    return lax.dot_general(a, b, (((da,), (db,)), ((), ())), preferred_element_type=f32)


def kernel(n_ctx, n_head, heads, *refs):
    (q_ref, k_ref, v_ref, taps_ref, gain_ref, g_ref,
     att_ref, gq_ref, gk_ref, gv_ref, gt_ref, gg_ref,
     tails, slope_q, slope_k, qf, kf, vf, gm, pb, sb, own, mixed, d0, dk, dv,
     acc_sq, acc_dot, inv_b, coef_b,
     u_out, u_in, t_out, t_in, w_out, w_in, r_out, r_in,
     lead_q, lead_q_in, lead_kv, lead_kv_in,
     part_a, part_b, rs_a, rs_b, own_a, own_b, ag_a, ag_b, stat, stat_in,
     s_tail, r_tail, s_u, r_u, s_t, r_t, s_w, r_w, s_r, r_r,
     s_lead, r_lead, s_stat, r_stat, s_rsa, r_rsa, s_rsb, r_rsb,
     s_aga, r_aga, s_agb, r_agb) = refs
    rows = q_ref.shape[0]
    width = heads * DH
    chunks = heads // GROUP
    pairs = n_ctx // 2
    me = lax.axis_index("ctx")
    head_me = lax.axis_index("head")
    pair = lax.div(me, 2)
    minor = lax.rem(me, 2)
    partner = pair * 2 + 1 - minor
    is_odd = minor.astype(f32)
    is_even = 1.0 - is_odd
    owners = min(n_ctx, width // 128)
    piece = width // owners

    barrier = pltpu.get_barrier_semaphore()

    def greet(i, _):
        pl.semaphore_signal(barrier, inc=1, device_id={"ctx": lax.rem(me + i, n_ctx)}, device_id_type=MESH)
        return 0

    lax.fori_loop(1, n_ctx, greet, 0)
    for i in range(1, n_head):
        pl.semaphore_signal(barrier, inc=1, device_id={"head": lax.rem(head_me + i, n_head)}, device_id_type=MESH)

    @pl.when(me == 0)
    def _():
        tails[...] = jnp.zeros_like(tails)

    @pl.when(me == n_ctx - 1)
    def _():
        lead_q_in[...] = jnp.zeros_like(lead_q_in)
        lead_kv_in[...] = jnp.zeros_like(lead_kv_in)

    @pl.when(pair == 0)
    def _():
        t_in[...] = jnp.zeros_like(t_in)

    @pl.when(pair == pairs - 1)
    def _():
        r_in[...] = jnp.zeros_like(r_in)

    part_a[...] = jnp.zeros_like(part_a)
    acc_sq[...] = jnp.zeros_like(acc_sq)
    acc_dot[...] = jnp.zeros_like(acc_dot)

    pl.semaphore_wait(barrier, n_ctx - 1 + n_head - 1)

    def send(src, dst, ssem, rsem, ctx):
        return pltpu.make_async_remote_copy(
            src_ref=src, dst_ref=dst, send_sem=ssem, recv_sem=rsem,
            device_id={"ctx": ctx}, device_id_type=MESH)

    following = lax.rem(me + 1, n_ctx)
    previous = lax.rem(me + n_ctx - 1, n_ctx)
    next_pair = lax.rem(me + 2, n_ctx)
    last_pair = lax.rem(me + n_ctx - 2, n_ctx)

    inputs = (q_ref, k_ref, v_ref)

    def tail_copy(m):
        return send(inputs[m].at[pl.ds(rows - TAIL, TAIL), :], tails.at[m], s_tail.at[m], r_tail.at[m], following)

    @pl.when(me < n_ctx - 1)
    def _():
        for m in range(3):
            tail_copy(m).start()

    @pl.when(me > 0)
    def _():
        for m in range(3):
            tail_copy(m).wait_recv()

    def lanes_of(h):
        return pl.ds(pl.multiple_of(h * DH, DH), DH)

    def shifted(m, lanes):
        ext = jnp.concatenate(
            [tails[m, :, lanes].astype(f32)[TAIL - 8:], inputs[m][:, lanes].astype(f32)], axis=0)
        return [ext[8 - (KS - 1) + j: 8 - (KS - 1) + j + rows] for j in range(KS)]

    def conv(m, lanes):
        xs = shifted(m, lanes)
        total = taps_ref[m, 0:1, lanes] * xs[0]
        for j in range(1, KS):
            total = total + taps_ref[m, j:j + 1, lanes] * xs[j]
        return total

    def taps_grad(m, lanes, d):
        return [jnp.sum(d * x, axis=0, keepdims=True) for x in shifted(m, lanes)]

    row_ids = lax.broadcasted_iota(jnp.int32, (rows, rows), 0)
    col_ids = lax.broadcasted_iota(jnp.int32, (rows, rows), 1)
    causal = row_ids >= col_ids

    def u_copy(c):
        return send(u_out.at[c], u_in.at[c], s_u.at[c], r_u.at[c], partner)

    def t_copy(c):
        return send(t_out.at[c], t_in.at[c], s_t.at[c], r_t.at[c], next_pair)

    def w_copy(c):
        return send(w_out.at[c], w_in.at[c], s_w.at[c], r_w.at[c], partner)

    def r_copy(c):
        return send(r_out.at[c], r_in.at[c], s_r.at[c], r_r.at[c], last_pair)

    def features(c, _):
        for i in range(GROUP):
            h = c * GROUP + i
            lanes = lanes_of(h)
            pre = conv(1, lanes)
            sig = 1.0 / (1.0 + jnp.exp(-pre))
            slope_k[:, lanes] = sig * (1.0 + pre * (1.0 - sig))
            kb = (pre * sig).astype(bf16)
            kf[:, lanes] = kb
            vb = conv(2, lanes).astype(bf16)
            vf[:, lanes] = vb
            state = dot(kb, vb, 0, 0)
            own[h] = state
            u_out[c, i] = state.astype(bf16)
        u_copy(c).start()
        return 0

    lax.fori_loop(0, chunks, features, 0)

    def within(c, _):
        for i in range(GROUP):
            h = c * GROUP + i
            lanes = lanes_of(h)
            pre = conv(0, lanes)
            sig = 1.0 / (1.0 + jnp.exp(-pre))
            slope_q[:, lanes] = sig * (1.0 + pre * (1.0 - sig))
            qb = (pre * sig).astype(bf16)
            qf[:, lanes] = qb
            weights = jnp.where(causal, dot(qb, kf[:, lanes], 1, 1), 0.0).astype(bf16)
            pb[h] = weights
            mixed[:, lanes] = dot(weights, vf[:, lanes], 1, 0)
        return 0

    lax.fori_loop(0, chunks, within, 0)

    def carried(c, _):
        u_copy(c).wait_recv()

        @pl.when(pair > 0)
        def _():
            t_copy(c).wait_recv()

        @pl.when(pair < pairs - 1)
        def _():
            for i in range(GROUP):
                t_out[c, i] = (t_in[c, i].astype(f32) + (u_in[c, i].astype(f32) + own[c * GROUP + i])).astype(t_out.dtype)
            t_copy(c).start()

        for i in range(GROUP):
            h = c * GROUP + i
            lanes = lanes_of(h)
            state = (t_in[c, i].astype(f32) + is_odd * u_in[c, i].astype(f32)).astype(bf16)
            sb[h] = state
            mix = mixed[:, lanes] + dot(qf[:, lanes], state, 1, 0)
            mixed[:, lanes] = mix
            acc_sq[...] += mix * mix
            acc_dot[...] += (gain_ref[:, lanes] * g_ref[:, lanes].astype(f32)) * mix
        return 0

    lax.fori_loop(0, chunks, carried, 0)

    stat[0:1, :] = jnp.sum(acc_sq[...].T, axis=0, keepdims=True)
    stat[1:2, :] = jnp.sum(acc_dot[...].T, axis=0, keepdims=True)
    stat[2:8, :] = jnp.zeros((6, rows), f32)

    def stat_copy(i):
        return pltpu.make_async_remote_copy(
            src_ref=stat, dst_ref=stat_in.at[i], send_sem=s_stat.at[i], recv_sem=r_stat.at[i],
            device_id={"head": lax.rem(head_me + i + 1, n_head)}, device_id_type=MESH)

    for i in range(n_head - 1):
        stat_copy(i).start()
    for i in range(n_head - 1):
        stat_copy(i).wait_recv()
    total = stat[...]
    for i in range(n_head - 1):
        total = total + stat_in[i]
    mean_sq = jnp.broadcast_to(total[0:1], (rows, rows)).T / W
    mean_dot = jnp.broadcast_to(total[1:2], (rows, rows)).T / W
    inverse = lax.rsqrt(mean_sq + EPSILON)
    inv_b[...] = inverse
    coef_b[...] = inverse * inverse * inverse * mean_dot

    def norm(c, _):
        for i in range(GROUP):
            h = c * GROUP + i
            lanes = lanes_of(h)
            mix = mixed[:, lanes]
            inv = inv_b[...]
            gain = gain_ref[:, lanes]
            up = g_ref[:, lanes].astype(f32)
            normed = mix * inv
            att_ref[:, lanes] = (normed * gain).astype(bf16)
            gmb = (inv * (gain * up) - mix * coef_b[...]).astype(bf16)
            gm[:, lanes] = gmb
            part_a[4:5, lanes] = jnp.sum(up * normed, axis=0, keepdims=True)
            state = dot(qf[:, lanes], gmb, 0, 0)
            own[h] = state
            w_out[c, i] = state.astype(bf16)
        w_copy(c).start()
        return 0

    lax.fori_loop(0, chunks, norm, 0)

    def local_grads(c, _):
        for i in range(GROUP):
            h = c * GROUP + i
            lanes = lanes_of(h)
            gmb = gm[:, lanes]
            dp = jnp.where(causal, dot(gmb, vf[:, lanes], 1, 1), 0.0).astype(bf16)
            dq = dot(dp, kf[:, lanes], 1, 0) + dot(gmb, sb[h], 1, 1)
            dq = dq * slope_q[:, lanes]
            d0[:, lanes] = dq
            lead_q[:, lanes] = dq[:8]
            for j, row in enumerate(taps_grad(0, lanes, dq)):
                part_a[j:j + 1, lanes] = row
            dk[:, lanes] = dot(dp, qf[:, lanes], 0, 0)
            dv[:, lanes] = dot(pb[h], gmb, 0, 0)
        return 0

    lax.fori_loop(0, chunks, local_grads, 0)

    def lead_copy(i):
        src, dst = ((lead_q, lead_q_in), (lead_kv, lead_kv_in))[i]
        return send(src, dst, s_lead.at[i], r_lead.at[i], previous)

    @pl.when(me > 0)
    def _():
        lead_copy(0).start()

    def span(o):
        return pl.ds(pl.multiple_of(o * piece, 128), piece)

    def rs_copy(i, part, held, ssem, rsem):
        to = lax.rem(me + i, n_ctx)
        return to, send(part.at[:, span(lax.rem(to, owners))], held.at[i], ssem.at[i], rsem.at[i], to)

    def rs_start(part, held, ssem, rsem):
        def one(i, _):
            to, copy = rs_copy(i, part, held, ssem, rsem)

            @pl.when(to < owners)
            def _():
                copy.start()
            return 0

        lax.fori_loop(1, n_ctx, one, 0)

    def ag_copy(i, mine, ag, ssem, rsem):
        to = lax.rem(me + i, n_ctx)
        return send(mine, ag.at[:, span(lax.rem(me, owners))], ssem.at[i], rsem.at[i], to)

    def rs_finish(part, held, ssem, rsem, mine, ag, ag_ssem, ag_rsem):
        @pl.when(me < owners)
        def _():
            mine[...] = part[:, span(me)]

            def one(i, _):
                rs_copy(i, part, held, ssem, rsem)[1].wait_recv()
                mine[...] += held[i]
                return 0

            lax.fori_loop(1, n_ctx, one, 0)

            def out(i, _):
                ag_copy(i, mine, ag, ag_ssem, ag_rsem).start()
                return 0

            lax.fori_loop(1, n_ctx, out, 0)
            ag[:, span(me)] = mine[...]

    def ag_finish(part, held, ssem, rsem, mine, ag, ag_ssem, ag_rsem):
        def one(i, _):
            @pl.when(lax.rem(me - i + n_ctx, n_ctx) < owners)
            def _():
                ag_copy(i, mine, ag, ag_ssem, ag_rsem).wait_recv()

            @pl.when(me < owners)
            def _():
                ag_copy(i, mine, ag, ag_ssem, ag_rsem).wait_send()

            @pl.when(lax.rem(me + i, n_ctx) < owners)
            def _():
                rs_copy(i, part, held, ssem, rsem)[1].wait_send()
            return 0

        lax.fori_loop(1, n_ctx, one, 0)

    set_a = (part_a, rs_a, s_rsa, r_rsa, own_a, ag_a, s_aga, r_aga)
    set_b = (part_b, rs_b, s_rsb, r_rsb, own_b, ag_b, s_agb, r_agb)
    rs_start(*set_a[:4])

    def state_grads(turn, _):
        c = turn
        w_copy(c).wait_recv()

        @pl.when(pair < pairs - 1)
        def _():
            r_copy(c).wait_recv()

        @pl.when(pair > 0)
        def _():
            for i in range(GROUP):
                r_out[c, i] = (r_in[c, i].astype(f32) + (w_in[c, i].astype(f32) + own[c * GROUP + i])).astype(r_out.dtype)
            r_copy(c).start()

        for i in range(GROUP):
            h = c * GROUP + i
            lanes = lanes_of(h)
            state = (r_in[c, i].astype(f32) + is_even * w_in[c, i].astype(f32)).astype(bf16)
            d1 = (dk[:, lanes] + dot(vf[:, lanes], state, 1, 1)) * slope_k[:, lanes]
            d2 = dv[:, lanes] + dot(kf[:, lanes], state, 1, 0)
            dk[:, lanes] = d1
            dv[:, lanes] = d2
            lead_kv[0, :, lanes] = d1[:8]
            lead_kv[1, :, lanes] = d2[:8]
            for m, d in ((1, d1), (2, d2)):
                for j, row in enumerate(taps_grad(m, lanes, d)):
                    part_b[(m - 1) * KS + j:(m - 1) * KS + j + 1, lanes] = row
        return 0

    lax.fori_loop(0, chunks, state_grads, 0)

    @pl.when(me > 0)
    def _():
        lead_copy(1).start()

    rs_start(*set_b[:4])
    rs_finish(*set_a)

    def conv_back(m, d_ref, lanes, ahead, out_ref):
        ext = jnp.concatenate([d_ref[:, lanes], ahead], axis=0)
        summed = taps_ref[m, 0:1, lanes] * ext[KS - 1:KS - 1 + rows]
        for j in range(1, KS):
            summed = summed + taps_ref[m, j:j + 1, lanes] * ext[KS - 1 - j:KS - 1 - j + rows]
        out_ref[:, lanes] = summed.astype(bf16)

    @pl.when(me < n_ctx - 1)
    def _():
        lead_copy(0).wait_recv()

    def back_q(h, _):
        lanes = lanes_of(h)
        conv_back(0, d0, lanes, lead_q_in[:, lanes], gq_ref)
        return 0

    lax.fori_loop(0, heads, back_q, 0)
    rs_finish(*set_b)

    @pl.when(me < n_ctx - 1)
    def _():
        lead_copy(1).wait_recv()

    def back_kv(h, _):
        lanes = lanes_of(h)
        conv_back(1, dk, lanes, lead_kv_in[0, :, lanes], gk_ref)
        conv_back(2, dv, lanes, lead_kv_in[1, :, lanes], gv_ref)
        return 0

    lax.fori_loop(0, heads, back_kv, 0)

    @pl.when(me < n_ctx - 1)
    def _():
        for m in range(3):
            tail_copy(m).wait_send()

    @pl.when(me > 0)
    def _():
        lead_copy(0).wait_send()
        lead_copy(1).wait_send()

    for i in range(n_head - 1):
        stat_copy(i).wait_send()

    def drain(c, _):
        u_copy(c).wait_send()
        w_copy(c).wait_send()

        @pl.when(pair < pairs - 1)
        def _():
            t_copy(c).wait_send()

        @pl.when(pair > 0)
        def _():
            r_copy(c).wait_send()
        return 0

    lax.fori_loop(0, chunks, drain, 0)
    ag_finish(*set_a)
    ag_finish(*set_b)
    scale = 1.0 / math.sqrt(rows * n_ctx)
    gt_ref[0] = ag_a[0:4, :] * scale
    gg_ref[...] = ag_a[4:5, :] * scale
    gt_ref[1] = ag_b[0:4, :] * scale
    gt_ref[2] = ag_b[4:8, :] * scale


def shards(n_ctx, n_head, query_in, key_in, value_in, conv_taps, norm_gain, cotangent):
    rows, width = query_in.shape
    heads = width // DH
    chunks = heads // GROUP
    owners = min(n_ctx, width // 128)
    piece = width // owners
    chain = bf16 if n_ctx <= 16 else f32
    vm = pltpu.VMEM
    dma = pltpu.SemaphoreType.DMA
    tile = (rows, width)
    states = (chunks, GROUP, DH, DH)
    scratch = [
        vm((3, TAIL, width), bf16), vm(tile, f32), vm(tile, f32),
        vm(tile, bf16), vm(tile, bf16), vm(tile, bf16), vm(tile, bf16),
        vm((heads, rows, rows), bf16), vm((heads, DH, DH), bf16), vm((heads, DH, DH), f32),
        vm(tile, f32), vm(tile, f32), vm(tile, f32), vm(tile, f32),
        vm((rows, DH), f32), vm((rows, DH), f32), vm((rows, rows), f32), vm((rows, rows), f32),
        vm(states, bf16), vm(states, bf16), vm(states, chain), vm(states, chain),
        vm(states, bf16), vm(states, bf16), vm(states, chain), vm(states, chain),
        vm((8, width), f32), vm((8, width), f32), vm((2, 8, width), f32), vm((2, 8, width), f32),
        vm((8, width), f32), vm((8, width), f32),
        vm((n_ctx, 8, piece), f32), vm((n_ctx, 8, piece), f32),
        vm((8, piece), f32), vm((8, piece), f32),
        vm((8, width), f32), vm((8, width), f32),
        vm((8, rows), f32), vm((n_head - 1, 8, rows), f32),
        dma((3,)), dma((3,)),
        dma((chunks,)), dma((chunks,)), dma((chunks,)), dma((chunks,)),
        dma((chunks,)), dma((chunks,)), dma((chunks,)), dma((chunks,)),
        dma((2,)), dma((2,)), dma((n_head - 1,)), dma((n_head - 1,)),
        dma((n_ctx,)), dma((n_ctx,)), dma((n_ctx,)), dma((n_ctx,)),
        dma((n_ctx,)), dma((n_ctx,)), dma((n_ctx,)), dma((n_ctx,)),
    ]
    block = pl.BlockSpec(memory_space=pltpu.VMEM)
    att, gq, gk, gv, gt, gg = pl.pallas_call(
        functools.partial(kernel, n_ctx, n_head, heads),
        out_shape=(
            jax.ShapeDtypeStruct(tile, bf16),
            jax.ShapeDtypeStruct(tile, bf16),
            jax.ShapeDtypeStruct(tile, bf16),
            jax.ShapeDtypeStruct(tile, bf16),
            jax.ShapeDtypeStruct((3, KS, width), f32),
            jax.ShapeDtypeStruct((1, width), f32),
        ),
        in_specs=[block] * 6,
        out_specs=(block,) * 6,
        scratch_shapes=scratch,
        compiler_params=pltpu.CompilerParams(
            collective_id=0, has_side_effects=True, vmem_limit_bytes=48 * 1024 * 1024),
        name="attend",
    )(query_in, key_in, value_in, conv_taps, norm_gain.reshape(1, width), cotangent)
    return att, gq, gk, gv, gt, gg.reshape(width)


def solution(mesh):
    tokens = P("ctx", "head")
    placed = (tokens, tokens, tokens, P(None, None, "head"), P("head"), tokens)
    return jax.shard_map(
        functools.partial(shards, mesh.shape["ctx"], mesh.shape["head"]),
        mesh=mesh,
        in_specs=placed,
        out_specs=(tokens, tokens, tokens, tokens, P(None, None, "head"), P("head")),
        check_vma=False,
    )
```
